32 devices in a mesh: gx: 4 (over z), gy: 4 (over x, core), gz: 2 (over y).
Axes of the slice: x: 2, y: 2, z: 4, core: 2. Of those that a mesh axis runs over, the one named last changes fastest.
Arguments:
- x_a: bfloat16 [32, 8, 64, 256], P(None, 'gx', 'gy', 'gz'), may hold values from -12 to 12
- x_b: bfloat16 [32, 8, 64, 256], P(None, 'gx', 'gy', 'gz'), may hold values from -12 to 12
- w_first: bfloat16 [3, 3, 3, 32, 32], replicated, may hold values from -0.21875 to 0.21875
- w_second: bfloat16 [3, 3, 3, 32, 32], replicated, may hold values from -0.21875 to 0.21875
- gain_first: float32 [32], replicated, may hold values from 0.1 to 1.9
- bias_first: float32 [32], replicated, may hold values from -2 to 2
- gain_second: float32 [32], replicated, may hold values from 0.1 to 1.9
- bias_second: float32 [32], replicated, may hold values from -2 to 2
- grad_out: bfloat16 [32, 8, 64, 256], P(None, 'gx', 'gy', 'gz'), may hold values from -6 to 6
Outputs:
- y_a: bfloat16 [32, 8, 64, 256], P(None, 'gx', 'gy', 'gz')
- dx_b: bfloat16 [32, 8, 64, 256], P(None, 'gx', 'gy', 'gz')
- grad_w_first: float32 [3, 3, 3, 32, 32], replicated
- grad_w_second: float32 [3, 3, 3, 32, 32], replicated
- grad_norm: float32 [4, 32], replicated
The draws below stay inside these ranges and needn't reach their ends.
All inputs are finite; a program needn't handle non-finite values.
Results may differ from the reference program's by a relative error of at most 0.0063.
Values may be sent and summed in bfloat16 or wider, within the bound.
A program may use at most 128 MiB of HBM per device.

```python
import math
import jax
import jax.numpy as jnp
from jax import lax

C = 32
NX = 8
NY = 64
NZ = 256
VOXELS = 131072


def draw_volume(key, salt):
    folded = jax.random.fold_in(key, salt)
    depth = jnp.arange(NX, dtype=jnp.float32) / max(NX - 1, 1)
    base = jnp.clip(jax.random.normal(folded, (C, NX, NY, NZ), jnp.float32), -4.0, 4.0)
    ramp = 1.0 + 2.0 * depth
    value = base * ramp[None, :, None, None]
    return value.astype(jnp.bfloat16)


def draw_x_a(key, part):
    return draw_volume(key, 11)


def draw_x_b(key, part):
    return draw_volume(key, 23)


def block_levels(key, extent, cuts, smallest, high):
    level = 1.0
    for axis_at, blocks in cuts:
        draws = jax.random.uniform(jax.random.fold_in(jax.random.fold_in(key, 6), axis_at), (blocks,), jnp.float32, smallest / len(cuts), high / len(cuts))
        level = level * jnp.repeat(jnp.exp(draws), extent[axis_at] // blocks).reshape((-1,) + (1,) * (len(extent) - 1 - axis_at))
    return level


def bell_draw(own_key, extent, scale, bound, cuts=(), kind=jnp.bfloat16):
    result = jax.random.normal(own_key, extent, jnp.float32) * scale
    if len(cuts) > 0:
        result = block_levels(own_key, extent, cuts, -0.22, 0.18) * result
    return jnp.clip(result, min=-bound, max=bound).astype(kind)


def setup_inputs(seed: int = 0) -> dict:
    arg_keys = jax.random.split(jax.random.key(seed), 10)
    return {
        "x_a": draw_x_a(jax.random.fold_in(arg_keys[9], 71), 0),
        "x_b": draw_x_b(jax.random.fold_in(arg_keys[9], 71), 0),
        "w_first": bell_draw(arg_keys[2], (3, 3, 3, C, C), (27 * C) ** -0.5, 0.21875),
        "w_second": bell_draw(arg_keys[3], (3, 3, 3, C, C), (27 * C) ** -0.5, 0.21875),
        "gain_first": jnp.clip(1.0 + 0.18 * jax.random.normal(arg_keys[4], (C,), jnp.float32), 0.1, 1.9),
        "bias_first": bell_draw(arg_keys[5], (C,), 0.5, 2.0, (), jnp.float32),
        "gain_second": jnp.clip(1.0 + 0.18 * jax.random.normal(arg_keys[6], (C,), jnp.float32), 0.1, 1.9),
        "bias_second": bell_draw(arg_keys[7], (C,), 0.5, 2.0, (), jnp.float32),
        "grad_out": bell_draw(arg_keys[8], (C, NX, NY, NZ), 1.0, 6.0, ((1, 4), (2, 4), (3, 2))),
    }


EPSILON = 1e-05

def spread(values):
    return values[:, None, None, None]

def silu_slope(value):
    sigma = jax.nn.sigmoid(value)
    return sigma * (1.0 + value * (1.0 - sigma))

def pad_volume(volume):
    return jnp.pad(volume, ((0, 0), (1, 1), (1, 1), (1, 1)))

def convolve(padded, weight):
    in_chan = padded.shape[0]
    out_chan = weight.shape[3]
    span_x = padded.shape[1] - 2
    span_y = padded.shape[2] - 2
    span_z = padded.shape[3] - 2
    total = jnp.zeros((out_chan, span_x * span_y * span_z), jnp.float32)
    for shift_x in range(3):
        for shift_y in range(3):
            pieces = [padded[:, shift_x:shift_x + span_x, shift_y:shift_y + span_y, shift_z:shift_z + span_z] for shift_z in range(3)]
            stacked = jnp.concatenate(pieces, axis=0).reshape(3 * in_chan, -1)
            matrix = weight[shift_x, shift_y].transpose(1, 0, 2).reshape(out_chan, 3 * in_chan)
            total = total + jnp.dot(matrix, stacked, preferred_element_type=jnp.float32)
    return total.reshape(out_chan, span_x, span_y, span_z)

def kernel_grad(padded, upstream):
    in_chan = padded.shape[0]
    out_chan = upstream.shape[0]
    span_x, span_y, span_z = (upstream.shape[1], upstream.shape[2], upstream.shape[3])
    flat = upstream.reshape(out_chan, -1)
    rows = []
    for shift_x in range(3):
        for shift_y in range(3):
            pieces = [padded[:, shift_x:shift_x + span_x, shift_y:shift_y + span_y, shift_z:shift_z + span_z] for shift_z in range(3)]
            stacked = jnp.concatenate(pieces, axis=0).reshape(3 * in_chan, -1)
            product = lax.dot_general(flat, stacked, (((1,), (1,)), ((), ())), preferred_element_type=jnp.float32)
            rows.append(product.reshape(out_chan, 3, in_chan).transpose(1, 0, 2))
    return jnp.stack(rows).reshape(3, 3, 3, out_chan, in_chan)

def flipped(weight):
    return jnp.flip(weight, (0, 1, 2)).transpose(0, 1, 2, 4, 3)

def forward_layer(features, weight, gain, bias):
    conv_out = convolve(pad_volume(features), weight)
    means = lax.optimization_barrier(jnp.sum(conv_out, axis=(1, 2, 3))) / VOXELS
    variance = lax.optimization_barrier(jnp.sum(jnp.square(conv_out - spread(means)), axis=(1, 2, 3))) / VOXELS
    scales = lax.rsqrt(variance + EPSILON)
    normed = (conv_out - spread(means)) * spread(scales)
    preact = spread(gain) * normed + spread(bias)
    output = (preact * jax.nn.sigmoid(preact)).astype(jnp.bfloat16)
    return (output, preact, normed, scales)

def backward_layer(upstream, preact, normed, scales, gain):
    slope = upstream * silu_slope(preact)
    sum_d = lax.optimization_barrier(jnp.sum(slope, axis=(1, 2, 3)))
    sum_dx = lax.optimization_barrier(jnp.sum(slope * normed, axis=(1, 2, 3)))
    delta = spread(gain * scales) * (slope - spread(sum_d / VOXELS) - normed * spread(sum_dx / VOXELS))
    return (delta.astype(jnp.bfloat16), sum_d, sum_dx)

def reference(x_a, x_b, w_first, w_second, gain_first, bias_first, gain_second, bias_second, grad_out):
    hidden_a = forward_layer(x_a, w_first, gain_first, bias_first)[0]
    y_a = forward_layer(hidden_a, w_second, gain_second, bias_second)[0]
    hidden_b, pre_one, norm_one, scale_one = forward_layer(x_b, w_first, gain_first, bias_first)
    unused, pre_two, norm_two, scale_two = forward_layer(hidden_b, w_second, gain_second, bias_second)
    factor = 1.0 / math.sqrt(VOXELS)
    delta_two, sum_d2, sum_x2 = backward_layer(grad_out.astype(jnp.float32), pre_two, norm_two, scale_two, gain_second)
    grad_w_second = kernel_grad(pad_volume(hidden_b), delta_two) * factor
    upstream_one = convolve(pad_volume(delta_two), flipped(w_second))
    delta_one, sum_d1, sum_x1 = backward_layer(upstream_one, pre_one, norm_one, scale_one, gain_first)
    grad_w_first = kernel_grad(pad_volume(x_b), delta_one) * factor
    dx_b = convolve(pad_volume(delta_one), flipped(w_first)).astype(jnp.bfloat16)
    grad_norm = jnp.stack([sum_x1, sum_d1, sum_x2, sum_d2]) * factor
    return (y_a, dx_b, grad_w_first, grad_w_second, grad_norm)
```

```python
import functools
import math

import jax
import jax.numpy as jnp
from jax import lax
from jax.experimental import pallas as pl
from jax.experimental.pallas import tpu as pltpu
from jax.sharding import PartitionSpec as P

EPSILON = 1e-05
AXES = ("gx", "gy", "gz")
MESH = pl.DeviceIdType.MESH


def slope_of(z):
    s = jax.nn.sigmoid(z)
    return s * (1.0 + z * (1.0 - s))


def kernel(
    sizes, voxels,
    xa, xb, go, w1, w2, w1t, w2t, g1, b1, g2, b2,
    ya, dxb, gw1, gw2, gnorm,
    pads, edge_out, edge_in, shift_a, shift_xb, shift_hb, shift_d,
    c1a, c1b, c2a, c2b, d2, d1, stat, wbuf, wacc,
    halo_send, halo_recv, sum_send, sum_recv, w_send, w_recv,
):
    nx, ny, chan, nz = xa.shape
    half = ny // 2
    wide = ny + 2
    me = [lax.axis_index(a) for a in AXES]
    factor = 1.0 / math.sqrt(voxels)
    lane = lax.broadcasted_iota(jnp.int32, (chan, nz), 1)
    zero = jnp.zeros((chan, nz), jnp.float32)

    def peers(k):
        n = sizes[k]
        return [(d, lax.rem(me[k] + d, n), lax.rem(me[k] + n - d, n)) for d in range(1, n)]

    barrier = pltpu.get_barrier_semaphore()
    count = 0
    for k in range(3):
        for _, to, _ in peers(k):
            pl.semaphore_signal(barrier, inc=1, device_id={AXES[k]: to}, device_id_type=MESH)
            count += 1
    pl.semaphore_wait(barrier, count)

    def halo_refs(v, k):
        p = pads.at[v]
        if k == 0:
            rows = pl.ds(1, ny)
            return (p.at[nx, rows], p.at[0, rows]), (p.at[1, rows], p.at[nx + 1, rows])
        if k == 1:
            return (p.at[:, ny], p.at[:, 0]), (p.at[:, 1], p.at[:, ny + 1])
        return (edge_out.at[v, 0], edge_in.at[v, 0]), (edge_out.at[v, 1], edge_in.at[v, 1])

    def halo_copy(v, k, side):
        src, dst = halo_refs(v, k)[side]
        return pltpu.make_async_remote_copy(
            src_ref=src, dst_ref=dst, send_sem=halo_send.at[v, k, side],
            recv_sem=halo_recv.at[v, k, side], device_id={AXES[k]: me[k] + 1 - 2 * side},
            device_id_type=MESH)

    def halo_start(v, k):
        n = sizes[k]
        (_, up_dst), (_, down_dst) = halo_refs(v, k)

        @pl.when(me[k] < n - 1)
        def _():
            halo_copy(v, k, 0).start()

        @pl.when(me[k] > 0)
        def _():
            halo_copy(v, k, 1).start()

        @pl.when(me[k] == 0)
        def _():
            up_dst[...] = jnp.zeros(up_dst.shape, up_dst.dtype)

        @pl.when(me[k] == n - 1)
        def _():
            down_dst[...] = jnp.zeros(down_dst.shape, down_dst.dtype)

    def halo_wait(v, k):
        n = sizes[k]

        @pl.when(me[k] < n - 1)
        def _():
            halo_copy(v, k, 0).wait_send()
            halo_copy(v, k, 1).wait_recv()

        @pl.when(me[k] > 0)
        def _():
            halo_copy(v, k, 1).wait_send()
            halo_copy(v, k, 0).wait_recv()

    def pack(v):
        def step(x, carry):
            low, high = carry
            for y in range(wide):
                tile = pads[v, x, y].astype(jnp.float32)
                here = lane == x * wide + y
                high = jnp.where(here, tile[:, nz - 1:nz], high)
                low = jnp.where(here, tile[:, 0:1], low)
            return low, high
        low, high = lax.fori_loop(0, nx + 2, step, (zero, zero))
        edge_out[v, 0] = high.astype(jnp.bfloat16)
        edge_out[v, 1] = low.astype(jnp.bfloat16)

    def unpack(v, shifted):
        low = edge_in[v, 0].astype(jnp.float32)
        high = pltpu.roll(edge_in[v, 1].astype(jnp.float32), nz - 1, 1)

        def step(x, carry):
            low, high = carry
            for y in range(wide):
                row = x * wide + y
                own = pads[v, x, y]
                tile = own.astype(jnp.float32)
                shifted[row, 0:chan] = jnp.where(
                    lane == 0, low, pltpu.roll(tile, 1, 1)).astype(jnp.bfloat16)
                shifted[row, chan:2 * chan] = own
                shifted[row, 2 * chan:] = jnp.where(
                    lane == nz - 1, high, pltpu.roll(tile, nz - 1, 1)).astype(jnp.bfloat16)
                low = pltpu.roll(low, nz - 1, 1)
                high = pltpu.roll(high, nz - 1, 1)
            return low, high
        lax.fori_loop(0, nx + 2, step, (low, high))

    def halo_rest(todo):
        for v, _ in todo:
            halo_wait(v, 0)
        for v, _ in todo:
            halo_start(v, 1)
        for v, _ in todo:
            halo_wait(v, 1)
        for v, _ in todo:
            pack(v)
            halo_start(v, 2)
        for v, _ in todo:
            halo_wait(v, 2)
        for v, shifted in todo:
            unpack(v, shifted)

    def stacked(shifted, x, y):
        parts = []
        for tx in range(3):
            for ty in range(3):
                row = (x + tx) * wide + y + ty
                parts.append(jnp.concatenate([shifted[row], shifted[row + 1]], axis=1))
        return jnp.concatenate(parts, axis=0)

    def place(i):
        return i // half, (i % half) * 2

    def row_loop(body, init):
        def step(i, carry):
            x, y = i // (ny // 4), (i % (ny // 4)) * 4
            for u in range(4):
                carry = body(x, y + u, carry)
            return carry
        return lax.fori_loop(0, nx * (ny // 4), step, init)

    def total(value):
        return jnp.sum(value, axis=1, keepdims=True)

    def tile_of(values):
        tile = zero
        for at, value in enumerate(values):
            tile = jnp.where(lane == at, value, tile)
        return tile

    def all_sum(slots, k, send, recv):
        def copy(at, to, frm):
            return pltpu.make_async_remote_copy(
                src_ref=slots.at[at], dst_ref=slots.at[at], send_sem=send.at[to],
                recv_sem=recv.at[at], device_id={AXES[k]: to}, device_id_type=MESH)

        def start():
            for _, to, frm in peers(k):
                copy(me[k], to, frm).start()

        def finish():
            for _, to, frm in peers(k):
                copy(me[k], to, frm).wait_send()
                copy(frm, to, frm).wait_recv()
        return start, finish

    def reduce_stats(j, tile):
        for k in range(3):
            slots = stat.at[j, k]
            slots[me[k]] = tile
            start, finish = all_sum(slots, k, sum_send.at[j, k], sum_recv.at[j, k])
            start()
            finish()
            tile = slots[0]
            for r in range(1, sizes[k]):
                tile = tile + slots[r]
        return tile

    def weight_start(j, k, value):
        slots = wbuf.at[j, k]
        slots[me[k]] = value.astype(jnp.bfloat16)
        all_sum(slots, k, w_send.at[j, k], w_recv.at[j, k])[0]()

    def weight_finish(j, k):
        slots = wbuf.at[j, k]
        all_sum(slots, k, w_send.at[j, k], w_recv.at[j, k])[1]()
        value = slots[0].astype(jnp.float32)
        for r in range(1, sizes[k]):
            value = value + slots[r].astype(jnp.float32)
        return value

    def conv_stats(shift_one, shift_two, w, out_one, out_two):
        def step(i, carry):
            x, y = place(i)
            new = []
            for n, (shifted, out) in enumerate(((shift_one, out_one), (shift_two, out_two))):
                o = jnp.dot(w[...], stacked(shifted, x, y), preferred_element_type=jnp.float32)
                left, right = o[:, :nz], o[:, nz:]
                out[x, y] = left
                out[x, y + 1] = right
                new.append(carry[2 * n] + left + right)
                new.append(carry[2 * n + 1] + left * left + right * right)
            return tuple(new)
        return lax.fori_loop(0, nx * half, step, (zero,) * 4)

    def norm(tile, at):
        mean = tile[:, at:at + 1] / voxels
        var = tile[:, at + 1:at + 2] / voxels - mean * mean
        return jnp.broadcast_to(mean, zero.shape), jnp.broadcast_to(
            lax.rsqrt(var + EPSILON), zero.shape)

    def wgrad(v, shifted):
        wacc[...] = jnp.zeros(wacc.shape, jnp.float32)

        def step(i, carry):
            x, y = place(i)
            delta = jnp.concatenate([pads[v, x + 1, y + 1], pads[v, x + 1, y + 2]], axis=1)
            wacc[...] += lax.dot_general(
                delta, stacked(shifted, x, y), (((1,), (1,)), ((), ())),
                preferred_element_type=jnp.float32)
            return carry
        lax.fori_loop(0, nx * half, step, 0)

    def fill(x, y, carry):
        pads[0, x + 1, y + 1] = xa[x, y]
        pads[1, x + 1, y + 1] = xb[x, y]
        return carry
    row_loop(fill, 0)
    halo_start(0, 0)
    halo_start(1, 0)
    halo_rest(((0, shift_a), (1, shift_xb)))
    sums = conv_stats(shift_a, shift_xb, w1, c1a, c1b)
    tile = reduce_stats(0, tile_of([total(s) for s in sums]))
    mean_a, scale_a = norm(tile, 0)
    mean_one, scale_one = norm(tile, 2)
    gain_one = jnp.broadcast_to(g1[...], zero.shape)
    bias_one = jnp.broadcast_to(b1[...], zero.shape)
    gain_two = jnp.broadcast_to(g2[...], zero.shape)
    bias_two = jnp.broadcast_to(b2[...], zero.shape)

    def silu(z):
        return (z * jax.nn.sigmoid(z)).astype(jnp.bfloat16)

    def hidden(x, y, carry):
        za = gain_one * ((c1a[x, y] - mean_a) * scale_a) + bias_one
        pads[2, x + 1, y + 1] = silu(za)
        nb = (c1b[x, y] - mean_one) * scale_one
        c1b[x, y] = nb
        pads[3, x + 1, y + 1] = silu(gain_one * nb + bias_one)
        return carry
    row_loop(hidden, 0)
    halo_start(2, 0)
    halo_start(3, 0)
    halo_rest(((2, shift_a), (3, shift_hb)))
    sums = conv_stats(shift_a, shift_hb, w2, c2a, c2b)
    tile = reduce_stats(1, tile_of([total(s) for s in sums]))
    mean_a2, scale_a2 = norm(tile, 0)
    mean_two, scale_two = norm(tile, 2)

    def slope_two(x, y, carry):
        sd, sx = carry
        nb = (c2b[x, y] - mean_two) * scale_two
        c2b[x, y] = nb
        d = go[x, y].astype(jnp.float32) * slope_of(gain_two * nb + bias_two)
        d2[x, y] = d
        return sd + d, sx + d * nb
    sd, sx = row_loop(slope_two, (zero, zero))
    tile2 = reduce_stats(2, tile_of([total(sx), total(sd)]))
    sx2 = jnp.broadcast_to(tile2[:, 0:1] / voxels, zero.shape)
    sd2 = jnp.broadcast_to(tile2[:, 1:2] / voxels, zero.shape)

    def delta_two(x, y, carry):
        pads[4, x + 1, y + 1] = ((gain_two * scale_two) * (
            d2[x, y] - sd2 - c2b[x, y] * sx2)).astype(jnp.bfloat16)
        return carry
    row_loop(delta_two, 0)
    halo_start(4, 0)
    wgrad(4, shift_hb)

    def finish_a(x, y, carry):
        ya[x, y] = silu(gain_two * ((c2a[x, y] - mean_a2) * scale_a2) + bias_two)
        return carry
    row_loop(finish_a, 0)
    halo_rest(((4, shift_d),))
    weight_start(0, 0, wacc[...])

    def back(i, carry):
        x, y = place(i)
        sd, sx = carry
        o = jnp.dot(w2t[...], stacked(shift_d, x, y), preferred_element_type=jnp.float32)
        for u in range(2):
            nb = c1b[x, y + u]
            d = o[:, u * nz:(u + 1) * nz] * slope_of(gain_one * nb + bias_one)
            d1[x, y + u] = d
            sd, sx = sd + d, sx + d * nb
        return sd, sx
    sd, sx = lax.fori_loop(0, nx * half, back, (zero, zero))
    weight_start(0, 1, weight_finish(0, 0))
    tile1 = reduce_stats(3, tile_of([total(sx), total(sd)]))
    sx1 = jnp.broadcast_to(tile1[:, 0:1] / voxels, zero.shape)
    sd1 = jnp.broadcast_to(tile1[:, 1:2] / voxels, zero.shape)
    gnorm[...] = tile_of(
        [tile1[:, 0:1], tile1[:, 1:2], tile2[:, 0:1], tile2[:, 1:2]]) * factor

    def delta_one(x, y, carry):
        pads[5, x + 1, y + 1] = ((gain_one * scale_one) * (
            d1[x, y] - sd1 - c1b[x, y] * sx1)).astype(jnp.bfloat16)
        return carry
    row_loop(delta_one, 0)
    halo_start(5, 0)
    wgrad(5, shift_xb)
    weight_start(0, 2, weight_finish(0, 1))
    halo_rest(((5, shift_d),))
    weight_start(1, 0, wacc[...])

    def last(i, carry):
        x, y = place(i)
        o = jnp.dot(w1t[...], stacked(shift_d, x, y), preferred_element_type=jnp.float32)
        for u in range(2):
            dxb[x, y + u] = o[:, u * nz:(u + 1) * nz].astype(jnp.bfloat16)
        return carry
    lax.fori_loop(0, nx * half, last, 0)
    weight_start(1, 1, weight_finish(1, 0))
    gw2[...] = weight_finish(0, 2) * factor
    weight_start(1, 2, weight_finish(1, 1))
    gw1[...] = weight_finish(1, 2) * factor


def body(sizes, x_a, x_b, w_first, w_second, gain_first, bias_first, gain_second, bias_second,
         grad_out):
    chan, nx, ny, nz = x_a.shape
    voxels = float(nx * ny * nz * math.prod(sizes))
    taps = 27 * chan

    def rows(block):
        return block.transpose(1, 2, 0, 3)

    def matrix(w):
        return w.reshape(27, chan, chan).transpose(1, 0, 2).reshape(chan, taps)

    def flipped(w):
        return jnp.flip(w, (0, 1, 2)).transpose(0, 1, 2, 4, 3)

    def column(v):
        return v.reshape(chan, 1)

    most = max(sizes)
    bf16, f32 = jnp.bfloat16, jnp.float32
    span = (nx + 2) * (ny + 2)
    grid = (nx, ny, chan, nz)
    vmem = pl.BlockSpec(memory_space=pltpu.VMEM)
    dma = pltpu.SemaphoreType.DMA
    y_a, dx_b, gw1, gw2, gnorm = pl.pallas_call(
        functools.partial(kernel, sizes, voxels),
        out_shape=(
            jax.ShapeDtypeStruct(grid, bf16),
            jax.ShapeDtypeStruct(grid, bf16),
            jax.ShapeDtypeStruct((chan, taps), f32),
            jax.ShapeDtypeStruct((chan, taps), f32),
            jax.ShapeDtypeStruct((chan, nz), f32),
        ),
        in_specs=[vmem] * 11,
        out_specs=[vmem] * 5,
        scratch_shapes=[
            pltpu.VMEM((6, nx + 2, ny + 2, chan, nz), bf16),
            pltpu.VMEM((6, 2, chan, nz), bf16),
            pltpu.VMEM((6, 2, chan, nz), bf16),
        ] + [pltpu.VMEM((span, 3 * chan, nz), bf16)] * 4
        + [pltpu.VMEM(grid, f32)] * 6
        + [
            pltpu.VMEM((4, 3, most, chan, nz), f32),
            pltpu.VMEM((2, 3, most, chan, taps), bf16),
            pltpu.VMEM((chan, taps), f32),
            dma((6, 3, 2)), dma((6, 3, 2)),
            dma((4, 3, most)), dma((4, 3, most)),
            dma((2, 3, most)), dma((2, 3, most)),
        ],
        compiler_params=pltpu.CompilerParams(
            collective_id=0, has_side_effects=True, vmem_limit_bytes=50 * 1024 * 1024),
    )(
        rows(x_a), rows(x_b), rows(grad_out),
        matrix(w_first), matrix(w_second), matrix(flipped(w_first)), matrix(flipped(w_second)),
        column(gain_first), column(bias_first), column(gain_second), column(bias_second),
    )

    def tensor(g):
        return g.reshape(chan, 27, chan).transpose(1, 0, 2).reshape(3, 3, 3, chan, chan)

    return (
        y_a.transpose(2, 0, 1, 3), dx_b.transpose(2, 0, 1, 3),
        tensor(gw1), tensor(gw2), gnorm[:, :4].T,
    )


def solution(mesh):
    sizes = tuple(mesh.shape[a] for a in AXES)
    split = P(None, *AXES)
    return jax.shard_map(
        functools.partial(body, sizes),
        mesh=mesh,
        in_specs=(split, split, P(), P(), P(), P(), P(), P(), split),
        out_specs=(split, split, P(), P(), P()),
        check_vma=False,
    )
```

```python
import functools
import math

import jax
import jax.numpy as jnp
from jax import lax
from jax.experimental import pallas as pl
from jax.experimental.pallas import tpu as pltpu
from jax.sharding import PartitionSpec as P

EPSILON = 1e-05
AXES = ("gx", "gy", "gz")
MESH = pl.DeviceIdType.MESH


def slope_of(z):
    s = jax.nn.sigmoid(z)
    return s * (1.0 + z * (1.0 - s))


def kernel(
    sizes, voxels,
    xa, xb, go, w1, w2, w1t, w2t, g1, b1, g2, b2,
    ya, dxb, gw1, gw2, gnorm,
    pads, edge_out, edge_in, edge_x, bases, shift_a, shift_xb, shift_hb, shift_d,
    c1a, c1b, c2a, c2b, d2, d1, stat, wbuf, wacc,
    halo_send, halo_recv, sum_send, sum_recv, w_send, w_recv,
):
    nx, ny, chan, nz = xa.shape
    half = ny // 2
    wide = ny + 2
    me = [lax.axis_index(a) for a in AXES]
    factor = 1.0 / math.sqrt(voxels)
    lane = lax.broadcasted_iota(jnp.int32, (chan, nz), 1)
    zero = jnp.zeros((chan, nz), jnp.float32)

    counts = (sizes[0], sizes[1] * sizes[2])
    rank = (me[0], me[1] * sizes[2] + me[2])

    def peers(k):
        n = counts[k]
        return [(lax.rem(rank[k] + d, n), lax.rem(rank[k] + n - d, n)) for d in range(1, n)]

    def where(k, at):
        if k == 0:
            return {AXES[0]: at}
        return {AXES[1]: at // sizes[2], AXES[2]: at % sizes[2]}

    barrier = pltpu.get_barrier_semaphore()
    count = 0
    for k in range(2):
        for to, _ in peers(k):
            pl.semaphore_signal(barrier, inc=1, device_id=where(k, to), device_id_type=MESH)
            count += 1
    pl.semaphore_wait(barrier, count)

    def halo_refs(v, k):
        p = pads.at[v]
        if k == 0:
            rows = pl.ds(1, ny)
            return (p.at[nx, rows], p.at[0, rows]), (p.at[1, rows], p.at[nx + 1, rows])
        if k == 1:
            rows = pl.ds(1, nx)
            return (p.at[rows, ny], p.at[rows, 0]), (p.at[rows, 1], p.at[rows, ny + 1])
        if k == 3 or k == 4:
            y = 0 if k == 3 else ny + 1
            return (p.at[nx, y], p.at[0, y]), (p.at[1, y], p.at[nx + 1, y])
        if k == 5:
            return (edge_in.at[v], edge_x.at[v, 0]), (edge_in.at[v], edge_x.at[v, 1])
        return (edge_out.at[v, 0], edge_in.at[v, 0]), (edge_out.at[v, 1], edge_in.at[v, 1])

    def halo_copy(v, k, side):
        src, dst = halo_refs(v, k)[side]
        return pltpu.make_async_remote_copy(
            src_ref=src, dst_ref=dst, send_sem=halo_send.at[v, k, side],
            recv_sem=halo_recv.at[v, k, side], device_id={AXES[along[k]]: me[along[k]] + 1 - 2 * side},
            device_id_type=MESH)

    along = (0, 1, 2, 0, 0, 0)

    def halo_start(v, k):
        here, n = me[along[k]], sizes[along[k]]
        (_, up_dst), (_, down_dst) = halo_refs(v, k)

        @pl.when(here < n - 1)
        def _():
            halo_copy(v, k, 0).start()

        @pl.when(here > 0)
        def _():
            halo_copy(v, k, 1).start()

        @pl.when(here == 0)
        def _():
            up_dst[...] = jnp.zeros(up_dst.shape, up_dst.dtype)

        @pl.when(here == n - 1)
        def _():
            down_dst[...] = jnp.zeros(down_dst.shape, down_dst.dtype)

    def halo_wait(v, k):
        here, n = me[along[k]], sizes[along[k]]

        @pl.when(here < n - 1)
        def _():
            halo_copy(v, k, 0).wait_send()
            halo_copy(v, k, 1).wait_recv()

        @pl.when(here > 0)
        def _():
            halo_copy(v, k, 1).wait_send()
            halo_copy(v, k, 0).wait_recv()

    def pack(v):
        def step(i, carry):
            low, high = carry
            x = i + 1
            for y in range(wide):
                tile = pads[v, x, y].astype(jnp.float32)
                here = lane == x * wide + y
                high = jnp.where(here, tile[:, nz - 1:nz], high)
                low = jnp.where(here, tile[:, 0:1], low)
            return low, high
        low, high = lax.fori_loop(0, nx, step, (zero, zero))
        edge_out[v, 0] = high.astype(jnp.bfloat16)
        edge_out[v, 1] = low.astype(jnp.bfloat16)

    def turned(tile, by):
        by = by % nz
        return pltpu.roll(tile, by, 1) if by else tile

    def unpack(v, shifted):
        for x in range(nx + 2):
            for side in range(2):
                if x == 0:
                    tile, at = edge_x[v, 0, side], nx * wide
                elif x == nx + 1:
                    tile, at = edge_x[v, 1, side], wide
                else:
                    tile, at = edge_in[v, side], x * wide
                bases[x, side] = turned(tile.astype(jnp.float32), -at - side)

        def step(x, carry):
            for y in range(wide):
                row = x * wide + y
                own = pads[v, x, y]
                tile = own.astype(jnp.float32)
                low = turned(bases[x, 0], -y)
                high = turned(bases[x, 1], -y)
                shifted[row, 0:chan] = jnp.where(
                    lane == 0, low, turned(tile, 1)).astype(jnp.bfloat16)
                shifted[row, chan:2 * chan] = own
                shifted[row, 2 * chan:] = jnp.where(
                    lane == nz - 1, high, turned(tile, -1)).astype(jnp.bfloat16)
            return carry
        lax.fori_loop(0, nx + 2, step, 0)

    def halo_rest(todo):
        for v, _ in todo:
            halo_wait(v, 1)
            halo_start(v, 3)
            halo_start(v, 4)
            pack(v)
            halo_start(v, 2)
        for v, _ in todo:
            halo_wait(v, 2)
            halo_start(v, 5)
        for v, shifted in todo:
            for k in (0, 3, 4, 5):
                halo_wait(v, k)
            unpack(v, shifted)

    def stacked(shifted, x, y):
        parts = []
        for tx in range(3):
            for ty in range(3):
                row = (x + tx) * wide + y + ty
                parts.append(jnp.concatenate([shifted[row], shifted[row + 1]], axis=1))
        return jnp.concatenate(parts, axis=0)

    def place(i):
        return i // half, (i % half) * 2

    def row_loop(body, init):
        def step(i, carry):
            x, y = i // (ny // 4), (i % (ny // 4)) * 4
            for u in range(4):
                carry = body(x, y + u, carry)
            return carry
        return lax.fori_loop(0, nx * (ny // 4), step, init)

    def total(value):
        return jnp.sum(value, axis=1, keepdims=True)

    def tile_of(values):
        tile = zero
        for at, value in enumerate(values):
            tile = jnp.where(lane == at, value, tile)
        return tile

    def all_sum(slots, k, send, recv):
        def copy(at, to, frm):
            return pltpu.make_async_remote_copy(
                src_ref=slots.at[at], dst_ref=slots.at[at], send_sem=send.at[to],
                recv_sem=recv.at[at], device_id=where(k, to), device_id_type=MESH)

        def start():
            for to, frm in peers(k):
                copy(rank[k], to, frm).start()

        def finish():
            for to, frm in peers(k):
                copy(rank[k], to, frm).wait_send()
                copy(frm, to, frm).wait_recv()
        return start, finish

    def reduce_stats(j, tile):
        for k in range(2):
            slots = stat.at[j, k]
            slots[rank[k]] = tile
            start, finish = all_sum(slots, k, sum_send.at[j, k], sum_recv.at[j, k])
            start()
            finish()
            tile = slots[0]
            for r in range(1, counts[k]):
                tile = tile + slots[r]
        return tile

    def weight_start(j, k, value):
        slots = wbuf.at[j, k]
        slots[rank[k]] = value.astype(jnp.bfloat16)
        all_sum(slots, k, w_send.at[j, k], w_recv.at[j, k])[0]()

    def weight_finish(j, k):
        slots = wbuf.at[j, k]
        all_sum(slots, k, w_send.at[j, k], w_recv.at[j, k])[1]()
        value = slots[0].astype(jnp.float32)
        for r in range(1, counts[k]):
            value = value + slots[r].astype(jnp.float32)
        return value

    def conv_stats(shift_one, shift_two, w, out_one, out_two):
        def step(i, carry):
            x, y = place(i)
            new = []
            for n, (shifted, out) in enumerate(((shift_one, out_one), (shift_two, out_two))):
                o = jnp.dot(w[...], stacked(shifted, x, y), preferred_element_type=jnp.float32)
                left, right = o[:, :nz], o[:, nz:]
                out[x, y] = left
                out[x, y + 1] = right
                new.append(carry[2 * n] + left + right)
                new.append(carry[2 * n + 1] + left * left + right * right)
            return tuple(new)
        return lax.fori_loop(0, nx * half, step, (zero,) * 4)

    def norm(tile, at):
        mean = tile[:, at:at + 1] / voxels
        var = tile[:, at + 1:at + 2] / voxels - mean * mean
        return jnp.broadcast_to(mean, zero.shape), jnp.broadcast_to(
            lax.rsqrt(var + EPSILON), zero.shape)

    def wgrad(v, shifted):
        wacc[...] = jnp.zeros(wacc.shape, jnp.float32)

        def step(i, carry):
            x, y = place(i)
            delta = jnp.concatenate([pads[v, x + 1, y + 1], pads[v, x + 1, y + 2]], axis=1)
            wacc[...] += lax.dot_general(
                delta, stacked(shifted, x, y), (((1,), (1,)), ((), ())),
                preferred_element_type=jnp.float32)
            return carry
        lax.fori_loop(0, nx * half, step, 0)

    def fill(x, y, carry):
        pads[0, x + 1, y + 1] = xa[x, y]
        pads[1, x + 1, y + 1] = xb[x, y]
        return carry
    row_loop(fill, 0)
    halo_start(0, 0)
    halo_start(0, 1)
    halo_start(1, 0)
    halo_start(1, 1)
    halo_rest(((0, shift_a), (1, shift_xb)))
    sums = conv_stats(shift_a, shift_xb, w1, c1a, c1b)
    tile = reduce_stats(0, tile_of([total(s) for s in sums]))
    mean_a, scale_a = norm(tile, 0)
    mean_one, scale_one = norm(tile, 2)
    gain_one = jnp.broadcast_to(g1[...], zero.shape)
    bias_one = jnp.broadcast_to(b1[...], zero.shape)
    gain_two = jnp.broadcast_to(g2[...], zero.shape)
    bias_two = jnp.broadcast_to(b2[...], zero.shape)

    def silu(z):
        return (z * jax.nn.sigmoid(z)).astype(jnp.bfloat16)

    def hidden(x, y, carry):
        za = gain_one * ((c1a[x, y] - mean_a) * scale_a) + bias_one
        pads[2, x + 1, y + 1] = silu(za)
        nb = (c1b[x, y] - mean_one) * scale_one
        c1b[x, y] = nb
        pads[3, x + 1, y + 1] = silu(gain_one * nb + bias_one)
        return carry
    row_loop(hidden, 0)
    halo_start(2, 0)
    halo_start(2, 1)
    halo_start(3, 0)
    halo_start(3, 1)
    halo_rest(((2, shift_a), (3, shift_hb)))
    sums = conv_stats(shift_a, shift_hb, w2, c2a, c2b)
    tile = reduce_stats(1, tile_of([total(s) for s in sums]))
    mean_a2, scale_a2 = norm(tile, 0)
    mean_two, scale_two = norm(tile, 2)

    def slope_two(x, y, carry):
        sd, sx = carry
        nb = (c2b[x, y] - mean_two) * scale_two
        c2b[x, y] = nb
        d = go[x, y].astype(jnp.float32) * slope_of(gain_two * nb + bias_two)
        d2[x, y] = d
        return sd + d, sx + d * nb
    sd, sx = row_loop(slope_two, (zero, zero))
    tile2 = reduce_stats(2, tile_of([total(sx), total(sd)]))
    sx2 = jnp.broadcast_to(tile2[:, 0:1] / voxels, zero.shape)
    sd2 = jnp.broadcast_to(tile2[:, 1:2] / voxels, zero.shape)

    def delta_two(x, y, carry):
        pads[4, x + 1, y + 1] = ((gain_two * scale_two) * (
            d2[x, y] - sd2 - c2b[x, y] * sx2)).astype(jnp.bfloat16)
        return carry
    row_loop(delta_two, 0)
    halo_start(4, 0)
    halo_start(4, 1)
    wgrad(4, shift_hb)

    def finish_a(x, y, carry):
        ya[x, y] = silu(gain_two * ((c2a[x, y] - mean_a2) * scale_a2) + bias_two)
        return carry
    row_loop(finish_a, 0)
    halo_rest(((4, shift_d),))
    weight_start(0, 0, wacc[...])

    def back(i, carry):
        x, y = place(i)
        sd, sx = carry
        o = jnp.dot(w2t[...], stacked(shift_d, x, y), preferred_element_type=jnp.float32)
        for u in range(2):
            nb = c1b[x, y + u]
            d = o[:, u * nz:(u + 1) * nz] * slope_of(gain_one * nb + bias_one)
            d1[x, y + u] = d
            sd, sx = sd + d, sx + d * nb
        return sd, sx
    sd, sx = lax.fori_loop(0, nx * half, back, (zero, zero))
    weight_start(0, 1, weight_finish(0, 0))
    tile1 = reduce_stats(3, tile_of([total(sx), total(sd)]))
    sx1 = jnp.broadcast_to(tile1[:, 0:1] / voxels, zero.shape)
    sd1 = jnp.broadcast_to(tile1[:, 1:2] / voxels, zero.shape)
    gnorm[...] = tile_of(
        [tile1[:, 0:1], tile1[:, 1:2], tile2[:, 0:1], tile2[:, 1:2]]) * factor

    def delta_one(x, y, carry):
        pads[5, x + 1, y + 1] = ((gain_one * scale_one) * (
            d1[x, y] - sd1 - c1b[x, y] * sx1)).astype(jnp.bfloat16)
        return carry
    row_loop(delta_one, 0)
    halo_start(5, 0)
    halo_start(5, 1)
    wgrad(5, shift_xb)
    halo_rest(((5, shift_d),))
    weight_start(1, 0, wacc[...])

    def last(i, carry):
        x, y = place(i)
        o = jnp.dot(w1t[...], stacked(shift_d, x, y), preferred_element_type=jnp.float32)
        for u in range(2):
            dxb[x, y + u] = o[:, u * nz:(u + 1) * nz].astype(jnp.bfloat16)
        return carry
    lax.fori_loop(0, nx * half, last, 0)
    weight_start(1, 1, weight_finish(1, 0))
    gw2[...] = weight_finish(0, 1) * factor
    gw1[...] = weight_finish(1, 1) * factor


def body(sizes, x_a, x_b, w_first, w_second, gain_first, bias_first, gain_second, bias_second,
         grad_out):
    chan, nx, ny, nz = x_a.shape
    voxels = float(nx * ny * nz * math.prod(sizes))
    taps = 27 * chan

    def rows(block):
        return block.transpose(1, 2, 0, 3)

    def matrix(w):
        return w.reshape(27, chan, chan).transpose(1, 0, 2).reshape(chan, taps)

    def flipped(w):
        return jnp.flip(w, (0, 1, 2)).transpose(0, 1, 2, 4, 3)

    def column(v):
        return v.reshape(chan, 1)

    most = max(sizes[0], sizes[1] * sizes[2])
    bf16, f32 = jnp.bfloat16, jnp.float32
    span = (nx + 2) * (ny + 2)
    grid = (nx, ny, chan, nz)
    vmem = pl.BlockSpec(memory_space=pltpu.VMEM)
    dma = pltpu.SemaphoreType.DMA
    y_a, dx_b, gw1, gw2, gnorm = pl.pallas_call(
        functools.partial(kernel, sizes, voxels),
        out_shape=(
            jax.ShapeDtypeStruct(grid, bf16),
            jax.ShapeDtypeStruct(grid, bf16),
            jax.ShapeDtypeStruct((chan, taps), f32),
            jax.ShapeDtypeStruct((chan, taps), f32),
            jax.ShapeDtypeStruct((chan, nz), f32),
        ),
        in_specs=[vmem] * 11,
        out_specs=[vmem] * 5,
        scratch_shapes=[
            pltpu.VMEM((6, nx + 2, ny + 2, chan, nz), bf16),
            pltpu.VMEM((6, 2, chan, nz), bf16),
            pltpu.VMEM((6, 2, chan, nz), bf16),
            pltpu.VMEM((6, 2, 2, chan, nz), bf16),
            pltpu.VMEM((nx + 2, 2, chan, nz), f32),
        ] + [pltpu.VMEM((span, 3 * chan, nz), bf16)] * 4
        + [pltpu.VMEM(grid, f32)] * 6
        + [
            pltpu.VMEM((4, 2, most, chan, nz), f32),
            pltpu.VMEM((2, 2, most, chan, taps), bf16),
            pltpu.VMEM((chan, taps), f32),
            dma((6, 6, 2)), dma((6, 6, 2)),
            dma((4, 2, most)), dma((4, 2, most)),
            dma((2, 2, most)), dma((2, 2, most)),
        ],
        compiler_params=pltpu.CompilerParams(
            collective_id=0, has_side_effects=True, vmem_limit_bytes=50 * 1024 * 1024),
    )(
        rows(x_a), rows(x_b), rows(grad_out),
        matrix(w_first), matrix(w_second), matrix(flipped(w_first)), matrix(flipped(w_second)),
        column(gain_first), column(bias_first), column(gain_second), column(bias_second),
    )

    def tensor(g):
        return g.reshape(chan, 27, chan).transpose(1, 0, 2).reshape(3, 3, 3, chan, chan)

    return (
        y_a.transpose(2, 0, 1, 3), dx_b.transpose(2, 0, 1, 3),
        tensor(gw1), tensor(gw2), gnorm[:, :4].T,
    )


def solution(mesh):
    sizes = tuple(mesh.shape[a] for a in AXES)
    split = P(None, *AXES)
    return jax.shard_map(
        functools.partial(body, sizes),
        mesh=mesh,
        in_specs=(split, split, P(), P(), P(), P(), P(), P(), split),
        out_specs=(split, split, P(), P(), P()),
        check_vma=False,
    )
```
